256 devices in a mesh: segment: 4 (over x), ctx: 32 (over y, z), tp: 2 (over core).
Axes of the slice: x: 4, y: 4, z: 8, core: 2. Of those that a mesh axis runs over, the one named last changes fastest.
Arguments:
- mamba_input: bfloat16 [4, 4096, 8192], P('segment', 'ctx', 'tp'), may hold values from -13 to 13
- mamba_gate: bfloat16 [4, 4096, 8192], P('segment', 'ctx', 'tp'), may hold values from -6 to 6
- step_size: bfloat16 [4, 4096, 128], P('segment', 'ctx', 'tp'), may hold values from 0 to 2, as said below
- state_maps: bfloat16 [4, 4096, 256], P('segment', 'ctx'), may hold values from -3 to 3
- decay_rate: float32 [128], P('tp'), may hold values from 0.5 to 2
- skip_gain: float32 [128], P('tp'), may hold values from 0.5 to 1.5
- norm_gain: float32 [8192], P('tp'), may hold values from 0.1 to 1.9
- queries: bfloat16 [4, 4096, 8192], P('segment', 'ctx', 'tp'), may hold values from -155 to 154
- keys: bfloat16 [4, 4096, 1024], P('segment', 'ctx', 'tp'), may hold values from -5 to 5
- values: bfloat16 [4, 4096, 1024], P('segment', 'ctx', 'tp'), may hold values from -6 to 6
- source_len: int32 [4], P('segment'), may hold values from 1638 to 3685
Outputs:
- mamba_handed: bfloat16 [4, 4096, 8192], P('segment', 'ctx', 'tp')
- attention_handed: bfloat16 [4, 4096, 8192], P('segment', 'ctx', 'tp')
The draws below stay inside these ranges and needn't reach their ends.
Inputs may be any that keep to these rules, and one draw needn't show every extreme that they name: `step_size`: positive.
All inputs are finite; a program needn't handle non-finite values.
Results may differ from the reference program's by a relative error of at most 0.0095.
Values may be sent and summed in bfloat16 or wider, within the bound.
A program may use at most 320 MiB of HBM per device.

```python
import math
import jax
import jax.numpy as jnp
from jax import lax

QUERY_HEADS = 64
KEY_VALUE_HEADS = 8
HEAD_WIDTH = 128
NST = 128
EM = 8192
HP = 64
MH = 128
MICRO_BATCHES = 4
SEQUENCE_TOKENS = 4096


def head_kinds(key):
    share = 4
    return jax.random.randint(jax.random.fold_in(key, 11), (MH,), 0, 8) < share


def rate_values(key):
    return jnp.exp(jax.random.uniform(jax.random.fold_in(key, 21), (MH,), jnp.float32, math.log(0.5), math.log(2.0)))


def draw_decay_rate(key, part):
    return rate_values(key)


def draw_step_size(key, part):
    speed_collection = rate_values(key)
    quick_route = head_kinds(key)
    rough = jnp.exp(jax.random.uniform(jax.random.fold_in(key, 31), (MICRO_BATCHES, SEQUENCE_TOKENS, MH), jnp.float32, math.log(0.5), math.log(2.0)))
    per_quick = jnp.exp(jax.random.uniform(jax.random.fold_in(key, 32), (MH,), jnp.float32, math.log(1.0 / 50.0), math.log(1.0 / 30.0)))
    whole_loss = jnp.exp(jax.random.uniform(jax.random.fold_in(key, 33), (MH,), jnp.float32, math.log(2.0), math.log(5.0)))
    base = jnp.where(quick_route, per_quick / speed_collection, whole_loss / (SEQUENCE_TOKENS * speed_collection))
    increment_collection = base[None, None, :] * rough
    spots = jax.random.randint(jax.random.fold_in(key, 34), (MICRO_BATCHES, 3, MH), 0, SEQUENCE_TOKENS)
    places = jnp.arange(SEQUENCE_TOKENS, dtype=jnp.int32)
    masked_indicators = jnp.any(places[None, :, None, None] == spots[:, None, :, :], axis=2)
    blend_coefficient = jax.random.uniform(jax.random.fold_in(key, 35), (MICRO_BATCHES, SEQUENCE_TOKENS, MH), jnp.float32, 0.22, 0.51)
    spike_collection = blend_coefficient / speed_collection[None, None, :]
    increment_collection = jnp.where(masked_indicators & jnp.logical_not(quick_route)[None, None, :], spike_collection, increment_collection)
    return increment_collection.astype(jnp.bfloat16)


def draw_mamba_input(key, part):
    channel = jnp.arange(EM, dtype=jnp.float32) / (EM - 1)
    spread = jnp.exp(jax.random.uniform(jax.random.fold_in(key, 52), (EM,), jnp.float32, math.log(0.7), math.log(1.4)))
    base = jnp.clip(jax.random.normal(jax.random.fold_in(key, 51), (MICRO_BATCHES, SEQUENCE_TOKENS, EM), jnp.float32), -5.0, 5.0)
    ramp = 0.6 * jnp.power(3.0, channel)
    return (base * ramp[None, None, :] * spread[None, None, :]).astype(jnp.bfloat16)


def attention_draw(key):
    query_base = jnp.clip(jax.random.normal(jax.random.fold_in(key, 41), (MICRO_BATCHES, SEQUENCE_TOKENS, QUERY_HEADS * HEAD_WIDTH), jnp.float32), -5.0, 5.0)
    key_offset = jnp.clip(jax.random.normal(jax.random.fold_in(key, 42), (MICRO_BATCHES, SEQUENCE_TOKENS, KEY_VALUE_HEADS * HEAD_WIDTH), jnp.float32), -5.0, 5.0)
    return (query_base, key_offset)


def draw_queries(key, part):
    return attention_draw(key)[0].astype(jnp.bfloat16)


def draw_keys(key, part):
    return attention_draw(key)[1].astype(jnp.bfloat16)


def with_ends(result, key, low, largest):
    extent = result.shape
    index_at = [jax.random.randint(jax.random.fold_in(key, axis), (), 0, extent[axis]) for axis in range(len(extent))]
    result = result.at[tuple(index_at)].set(low)
    longest = extent.index(max(extent))
    index_at[longest] = (index_at[longest] + 1) % extent[longest]
    return result.at[tuple(index_at)].set(largest)


def block_levels(rng, extent, shards, smallest, top_value):
    loudness = 1.0
    for dim, shards_of in shards:
        heights = jax.random.uniform(jax.random.fold_in(jax.random.fold_in(rng, 6), dim), (shards_of,), jnp.float32, smallest / len(shards), top_value / len(shards))
        loudness = loudness * jnp.repeat(jnp.exp(heights), extent[dim] // shards_of).reshape((-1,) + (1,) * (len(extent) - 1 - dim))
    return loudness


def noise(key, extent, width, most, shards=(), kind=jnp.bfloat16):
    array = jax.random.normal(key, extent, jnp.float32) * width
    if len(shards) > 0:
        array = block_levels(key, extent, shards, -0.22, 0.18) * array
    return jnp.clip(array, min=-most, max=most).astype(kind)


def setup_inputs(seed: int = 0) -> dict:
    arg_keys = jax.random.split(jax.random.key(seed), 12)
    return {
        "mamba_input": draw_mamba_input(jax.random.fold_in(arg_keys[11], 71), 0),
        "mamba_gate": noise(arg_keys[1], (MICRO_BATCHES, SEQUENCE_TOKENS, EM), 1.0, 6.0, ((0, 4), (1, 32), (2, 2))),
        "step_size": draw_step_size(jax.random.fold_in(arg_keys[11], 71), 0),
        "state_maps": noise(arg_keys[3], (MICRO_BATCHES, SEQUENCE_TOKENS, 2 * NST), 0.6, 3.0, ((0, 4), (1, 32))),
        "decay_rate": draw_decay_rate(jax.random.fold_in(arg_keys[11], 71), 0),
        "skip_gain": jnp.clip(jnp.exp(math.log(1.5) - 1.0986123 * jax.random.uniform(arg_keys[5], (MH,), jnp.float32) ** block_levels(arg_keys[5], (MH,), ((0, 2),), -0.2, 0.2)), 0.5, 1.5),
        "norm_gain": jnp.clip(1.0 + 0.18 * jax.random.normal(arg_keys[6], (EM,), jnp.float32), 0.1, 1.9),
        "queries": draw_queries(jax.random.fold_in(arg_keys[11], 71), 0),
        "keys": draw_keys(jax.random.fold_in(arg_keys[11], 71), 0),
        "values": noise(arg_keys[9], (MICRO_BATCHES, SEQUENCE_TOKENS, KEY_VALUE_HEADS * HEAD_WIDTH), 1.0, 6.0, ((0, 4), (1, 32), (2, 2))),
        "source_len": with_ends(jax.random.randint(arg_keys[10], (MICRO_BATCHES,), SEQUENCE_TOKENS * 2 // 5, SEQUENCE_TOKENS * 9 // 10), jax.random.fold_in(arg_keys[10], 1), SEQUENCE_TOKENS * 2 // 5, (SEQUENCE_TOKENS * 9 // 10) - 1).astype(jnp.int32),
    }


precise = lax.Precision.HIGHEST

def mamba_one(mixer_in, gate_in, step_in, maps_in, decay_rate, skip_gain, norm_gain):
    x_heads = mixer_in.astype(jnp.float32).reshape(SEQUENCE_TOKENS, MH, HP)
    increment_collection = step_in.astype(jnp.float32)
    b_rows = maps_in[:, :NST].astype(jnp.float32)
    c_rows = maps_in[:, NST:].astype(jnp.float32)

    def advance(state, inputs):
        x_now, step_now, b_now, c_now = inputs
        state = jnp.exp(-decay_rate * step_now)[:, None, None] * state + step_now[:, None, None] * b_now[None, :, None] * x_now[:, None, :]
        present_result = jnp.einsum('n,hnp->hp', c_now, state, precision=precise) + skip_gain[:, None] * x_now
        return (state, present_result)
    start_state = jnp.zeros((MH, NST, HP), jnp.float32)
    _, outputs = lax.scan(advance, start_state, (x_heads, increment_collection, b_rows, c_rows))
    raw = outputs.reshape(SEQUENCE_TOKENS, EM).astype(jnp.bfloat16)
    gated = raw.astype(jnp.float32) * jax.nn.silu(gate_in.astype(jnp.float32))
    mean_sq = lax.optimization_barrier(jnp.mean(gated * gated, axis=-1))
    return (gated * lax.rsqrt(mean_sq + 1e-05)[:, None] * norm_gain[None, :]).astype(jnp.bfloat16)

def attention_one(query_matrix, key_matrix, content_array, source):
    group_width = QUERY_HEADS // KEY_VALUE_HEADS
    query_head_rows = query_matrix.astype(jnp.float32).reshape(SEQUENCE_TOKENS, KEY_VALUE_HEADS, group_width, HEAD_WIDTH).transpose(1, 0, 2, 3)
    key_head_rows = key_matrix.astype(jnp.float32).reshape(SEQUENCE_TOKENS, KEY_VALUE_HEADS, HEAD_WIDTH).transpose(1, 0, 2)
    value_head_rows = content_array.astype(jnp.float32).reshape(SEQUENCE_TOKENS, KEY_VALUE_HEADS, HEAD_WIDTH).transpose(1, 0, 2)
    rows_per = math.gcd(512, SEQUENCE_TOKENS)
    count = SEQUENCE_TOKENS // rows_per
    positions = jnp.arange(SEQUENCE_TOKENS, dtype=jnp.int32)
    scale = 1.0 / math.sqrt(HEAD_WIDTH)

    def per_head(operands):
        q_head, k_head, v_head = operands

        def per_block(block_idx):
            start = block_idx * rows_per
            q_block = lax.dynamic_slice_in_dim(q_head, start, rows_per, 0)
            scores = jnp.einsum('tgd,sd->gts', q_block, k_head, precision=precise) * scale
            query_pos = start + positions[:rows_per]
            visible = (positions[None, :] <= query_pos[:, None]) | (positions[None, :] < source)
            scores = jnp.where(visible[None], scores, -jnp.inf)
            top = lax.optimization_barrier(jnp.max(scores, axis=-1, keepdims=True))
            weights = jnp.exp(scores - top)
            totals = lax.optimization_barrier(jnp.sum(weights, axis=-1))
            rounded = weights.astype(jnp.bfloat16).astype(jnp.float32)
            mixed = jnp.einsum('gts,sd->tgd', rounded, v_head, precision=precise)
            return mixed / jnp.transpose(totals)[:, :, None]
        blocks_out = lax.map(per_block, jnp.arange(count, dtype=jnp.int32))
        return blocks_out.reshape(SEQUENCE_TOKENS, group_width, HEAD_WIDTH)
    heads_out = lax.map(per_head, (query_head_rows, key_head_rows, value_head_rows))
    return heads_out.transpose(1, 0, 2, 3).reshape(SEQUENCE_TOKENS, QUERY_HEADS * HEAD_WIDTH).astype(jnp.bfloat16)

def reference(mamba_input, mamba_gate, step_size, state_maps, decay_rate, skip_gain, norm_gain, queries, keys, values, source_len):
    mamba_list = []
    attention_list = []
    for member in range(MICRO_BATCHES):
        mamba_list.append(mamba_one(mamba_input[member], mamba_gate[member], step_size[member], state_maps[member], decay_rate, skip_gain, norm_gain))
        attention_list.append(attention_one(queries[member], keys[member], values[member], source_len[member]))
    mamba_all = jnp.stack(mamba_list, axis=0)
    attention_all = jnp.stack(attention_list, axis=0)
    return (jnp.roll(mamba_all, 1, axis=0), jnp.roll(attention_all, 1, axis=0))
```

```python
import functools
import math

import jax
import jax.numpy as jnp
from jax import lax
from jax.experimental import pallas as pl
from jax.experimental.pallas import tpu as pltpu
from jax.sharding import PartitionSpec as P

QUERY_HEADS = 64
KEY_VALUE_HEADS = 8
GROUP = QUERY_HEADS // KEY_VALUE_HEADS
D = 128
NST = 128
HP = 64
Z_RING = 8
MESH = pl.DeviceIdType.MESH
NEG = -1e30
HIGH = lax.Precision.HIGHEST
F32 = jnp.float32
BF16 = jnp.bfloat16


def nt_dot(a, b):
    return lax.dot_general(a, b, (((1,), (1,)), ((), ())), preferred_element_type=F32)


def section_kernel(
    dims,
    x_ref, gate_ref, step_ref, maps_ref, rate_ref, skip_ref, gain_ref, q_ref, k_ref, v_ref, src_ref,
    mo_ref, ao_ref,
    kv, qb, sb, inbox, so, sin, yb, cum_e, ecum_e, tail_e, cum_t, dt_t, gram,
    sc, lim, mx, ls, acc, ob, mob, sqs, sqr,
    yk_send, yk_recv, q_send, q_recv, loc, ring_send, ring_recv, s_send, s_recv, r_send, r_recv,
    ao_send, ao_recv, mo_send, mo_recv, sq_send, sq_recv,
):
    nx, ny, nz, T, em = dims
    nc = ny * nz
    seg = lax.axis_index("segment")
    me = lax.axis_index("ctx")
    tp = lax.axis_index("tp")
    y = me // nz
    z = lax.rem(me, nz)
    after = lax.rem(seg + 1, nx)
    before = lax.rem(seg + nx - 1, nx)
    half = nz // 2

    def remote(src, dst, ssem, rsem, dev):
        return pltpu.make_async_remote_copy(
            src_ref=src, dst_ref=dst, send_sem=ssem, recv_sem=rsem, device_id=dev, device_id_type=MESH
        )

    def at_ctx(c):
        return (seg, c, tp)

    barrier = pltpu.get_barrier_semaphore()

    @pl.loop(1, nc)
    def _(i):
        pl.semaphore_signal(barrier, inc=1, device_id=at_ctx(lax.rem(me + i, nc)), device_id_type=MESH)

    for i in range(ny):
        pl.semaphore_signal(barrier, inc=1, device_id=(before, i * nz + z, tp), device_id_type=MESH)
    pl.semaphore_signal(barrier, inc=1, device_id=(seg, me, 1 - tp), device_id_type=MESH)
    pl.semaphore_wait(barrier, nc - 1 + ny + 1)

    def col(i, w):
        return pl.ds(pl.multiple_of(i * w, w), w)

    def yk_copy(i, kvi, src):
        o = lax.rem(y + i, ny)
        return remote(
            src.at[:, col(o, D)], kv.at[z, kvi, pl.ds(pl.multiple_of(y * T, T), T)],
            yk_send.at[i, kvi], yk_recv.at[i, kvi], at_ctx(o * nz + z),
        )

    def q_copy(i):
        o = lax.rem(y + i, ny)
        return remote(
            q_ref.at[:, col(o, GROUP * D)], qb.at[y], q_send.at[i], q_recv.at[i], at_ctx(o * nz + z)
        )

    for i in range(1, ny):
        yk_copy(i, 0, k_ref).start()
        yk_copy(i, 1, v_ref).start()
    own = [
        pltpu.make_async_copy(k_ref.at[:, col(y, D)], kv.at[z, 0, pl.ds(pl.multiple_of(y * T, T), T)], loc.at[0]),
        pltpu.make_async_copy(v_ref.at[:, col(y, D)], kv.at[z, 1, pl.ds(pl.multiple_of(y * T, T), T)], loc.at[1]),
        pltpu.make_async_copy(q_ref.at[:, col(y, GROUP * D)], qb.at[y], loc.at[2]),
    ]
    for c in own:
        c.start()

    heads = em // HP
    row = lax.broadcasted_iota(jnp.int32, (T, T), 0)
    lane = lax.broadcasted_iota(jnp.int32, (T, T), 1)
    low = (row >= lane)
    dt = step_ref[...].astype(F32)
    logs = -rate_ref[...] * dt
    cum = jnp.dot(low.astype(F32), logs, precision=HIGH, preferred_element_type=F32)
    last = cum[T - 1:T, :]
    tail = jnp.exp(last - cum) * dt
    ecum = jnp.exp(cum)
    cum_t[...] = cum.T
    dt_t[...] = dt.T
    width = min(512, em)
    for j in range(em // width):
        hrow = lax.broadcasted_iota(jnp.int32, (heads, width), 0)
        hcol = lax.broadcasted_iota(jnp.int32, (heads, width), 1)
        pick = (hrow == (hcol + j * width) // HP).astype(F32)
        sl = slice(j * width, (j + 1) * width)
        tail_e[:, sl] = jnp.dot(tail, pick, precision=HIGH, preferred_element_type=F32)
        cum_e[:, sl] = jnp.dot(cum, pick, precision=HIGH, preferred_element_type=F32)
        ecum_e[:, sl] = jnp.dot(ecum, pick, precision=HIGH, preferred_element_type=F32)

    right = at_ctx(y * nz + lax.rem(z + 1, nz))
    left = at_ctx(y * nz + lax.rem(z + nz - 1, nz))

    def ring_copy(b, kvi, way):
        return remote(
            kv.at[b, kvi], kv.at[b, kvi], ring_send.at[way, b, kvi], ring_recv.at[b, kvi],
            right if way == 0 else left,
        )

    reach = [[half, half - 1], [half - 1, half]]

    def ring_step(s):
        for kvi in range(2):
            for way in range(2):
                b = lax.rem(z + nz - s, nz) if way == 0 else lax.rem(z + s, nz)
                if 0 < s <= reach[way][kvi]:
                    ring_copy(b, kvi, way).wait_recv()
                if s < reach[way][kvi]:
                    ring_copy(b, kvi, way).start()

    for i in range(1, ny):
        yk_copy(i, 0, k_ref).wait_recv()
        yk_copy(i, 1, v_ref).wait_recv()
    own[0].wait()
    own[1].wait()
    ring_step(0)

    b_mat = maps_ref[:, :NST]
    c_mat = maps_ref[:, NST:]
    gram[...] = jnp.where(low, nt_dot(c_mat, b_mat), 0.0)
    b_t = b_mat.astype(F32).T.astype(BF16)
    sub16 = lax.broadcasted_iota(jnp.int32, (16, D), 0)

    def state_copy(i, p):
        return remote(sb.at[p], inbox.at[me], s_send.at[i], s_recv.at[me], at_ctx(p))

    def state_of(p):
        scaled = (x_ref[:, col(p, 128)].astype(F32) * tail_e[:, col(p, 128)]).astype(BF16)
        chunk = jnp.dot(b_t, scaled, preferred_element_type=F32)
        decay = ecum_e[T - 1:T, col(p, 128)]
        high = decay.astype(BF16).astype(F32)
        rest = jnp.where(sub16 < 8, high, decay - high)
        return chunk.astype(BF16), rest.astype(BF16)

    @pl.loop(1, nc)
    def _(i):
        p = lax.rem(me + i, nc)
        chunk, rest = state_of(p)
        sb[p, 0:NST] = chunk
        sb[p, NST:NST + 16] = rest
        state_copy(i, p).start()

    chunk, rest = state_of(me)
    inbox[me, 0:NST] = chunk
    inbox[me, NST:NST + 16] = rest

    for i in range(1, ny):
        q_copy(i).start()
    ring_step(1)

    def inner(p):
        xt = x_ref[:, col(p, 128)]
        ce = cum_e[:, col(p, 128)]
        g = gram[...]
        outs = []
        for k in range(2):
            diff = ce[:, k * HP:k * HP + 1] - cum_t[pl.ds(2 * p + k, 1), :]
            w = g * jnp.exp(jnp.minimum(diff, 0.0)) * dt_t[pl.ds(2 * p + k, 1), :]
            outs.append(jnp.dot(w.astype(BF16), xt, preferred_element_type=F32))
        mixed = jnp.where(lane < HP, outs[0], outs[1])
        yb[:, col(p, 128)] = mixed + skip_ref[:, col(p, 128)] * xt.astype(F32)

    parts = max(1, half - 1)
    for s in range(parts):
        @pl.loop(s * nc // parts, (s + 1) * nc // parts)
        def _(p):
            inner(p)
        ring_step(s + 2)

    def back_copy(c):
        return remote(so.at[c], sin.at[me], r_send.at[c], r_recv.at[me], at_ctx(c))

    def wait_state(c):
        remote(sb.at[0], inbox.at[c], s_send.at[0], s_recv.at[c], at_ctx(c)).wait_recv()

    def scan_step(c, carry):
        @pl.when(c != me)
        def _():
            wait_state(c)
        so[c] = carry.astype(BF16)

        @pl.when(c != me)
        def _():
            back_copy(c).start()
        @pl.when(c == me)
        def _():
            sin[me] = carry.astype(BF16)
        rest = inbox[c, NST:NST + 16].astype(F32)
        return carry * (rest[0:1] + rest[8:9]) + inbox[c, 0:NST].astype(F32)

    lax.fori_loop(0, nc, scan_step, jnp.zeros((NST, 128), F32))

    own[2].wait()
    for i in range(1, ny):
        q_copy(i).wait_recv()
    source = src_ref[0]
    scale2 = 1.0 / math.sqrt(D) * math.log2(math.e)
    R = 2 * T
    tiles = GROUP // 2
    keys = ny * T
    lane_k = lax.broadcasted_iota(jnp.int32, (R, T), 1)

    def out_copy(c):
        return remote(
            ob.at[c], ao_ref.at[:, col(y, GROUP * D)], ao_send.at[c], ao_recv.at[y],
            (after, c * nz + z, tp),
        )

    def attend(c):
        pos = c * (nz * T) + z * T + lax.rem(lax.broadcasted_iota(jnp.int32, (R, T), 0), T)
        lim[...] = jnp.maximum(pos + 1, source)
        for t in range(tiles):
            cols = [slice((2 * t + k) * D, (2 * t + k + 1) * D) for k in range(2)]
            q = jnp.concatenate([qb[c, :, cols[0]], qb[c, :, cols[1]]], axis=0)
            mx[...] = jnp.full((R, T), NEG, F32)

            @pl.loop(0, nz)
            def _(b):
                s = nt_dot(q, kv[b, 0])
                top = mx[...]
                for j in range(ny):
                    part = s[:, j * T:(j + 1) * T]
                    if j > 0:
                        part = jnp.where(lane_k + (j * nz * T + b * T) < lim[...], part, NEG)
                    sc[b, :, j * T:(j + 1) * T] = part
                    top = jnp.maximum(top, part)
                mx[...] = top

            m = jnp.max(mx[...], axis=-1, keepdims=True)
            acc[...] = jnp.zeros((R, D), F32)
            ls[...] = jnp.zeros((R, T), F32)

            @pl.loop(0, nz)
            def _(b):
                w = jnp.exp2((sc[b] - m) * scale2)
                total = ls[...]
                for j in range(ny):
                    total = total + w[:, j * T:(j + 1) * T]
                ls[...] = total
                acc[...] += jnp.dot(w.astype(BF16), kv[b, 1], preferred_element_type=F32)

            den = jnp.sum(ls[...], axis=-1, keepdims=True)
            o = (acc[...] / den).astype(BF16)
            ob[c, :, cols[0]] = o[:T]
            ob[c, :, cols[1]] = o[T:]
        out_copy(c).start()

    def sq_copy():
        return remote(sqs, sqr, sq_send, sq_recv, (seg, me, 1 - tp))

    mcols = min(1024, em)

    def mo_copy(j):
        return remote(
            mob.at[:, col(j, mcols)], mo_ref.at[:, col(j, mcols)], mo_send.at[j], mo_recv.at[j], (after, me, tp)
        )

    def finish():
        def step(p, sq):
            @pl.when(p != me)
            def _():
                remote(so.at[0], sin.at[p], r_send.at[0], r_recv.at[p], at_ctx(p)).wait_recv()
            entered = jnp.dot(c_mat, sin[p], preferred_element_type=F32)
            raw = (yb[:, col(p, 128)] + ecum_e[:, col(p, 128)] * entered).astype(BF16).astype(F32)
            g = gate_ref[:, col(p, 128)].astype(F32)
            gated = raw * (g / (1.0 + jnp.exp(-g)))
            yb[:, col(p, 128)] = gated
            return sq + gated * gated
        sqs[...] = lax.fori_loop(0, nc, step, jnp.zeros((T, 128), F32))
        sq_copy().start()
        sq_copy().wait_recv()
        total = jnp.sum(sqs[...] + sqr[...], axis=-1, keepdims=True)
        factor = lax.rsqrt(total / (2 * em) + 1e-5)
        for j in range(em // mcols):
            @pl.loop(0, mcols // 128)
            def _(i):
                p = j * (mcols // 128) + i
                mob[:, col(p, 128)] = (yb[:, col(p, 128)] * factor * gain_ref[:, col(p, 128)]).astype(BF16)
            mo_copy(j).start()

    early = ny - 1
    @pl.loop(0, early)
    def _(c):
        attend(c)
    finish()
    @pl.loop(early, ny)
    def _(c):
        attend(c)

    for i in range(1, ny):
        yk_copy(i, 0, k_ref).wait_send()
        yk_copy(i, 1, v_ref).wait_send()
        q_copy(i).wait_send()
    for s in range(half):
        for kvi in range(2):
            for way in range(2):
                b = lax.rem(z + nz - s, nz) if way == 0 else lax.rem(z + s, nz)
                if s < reach[way][kvi]:
                    ring_copy(b, kvi, way).wait_send()

    @pl.loop(1, nc)
    def _(i):
        p = lax.rem(me + i, nc)
        state_copy(i, p).wait_send()
        back_copy(p).wait_send()

    sq_copy().wait_send()
    for c in range(ny):
        out_copy(c).wait_send()
    for j in range(em // mcols):
        mo_copy(j).wait_send()
        mo_copy(j).wait_recv()
    for c in range(ny):
        remote(ob.at[0], ao_ref.at[:, col(c, GROUP * D)], ao_send.at[0], ao_recv.at[c], (after, me, tp)).wait_recv()


def on_device(mamba_input, mamba_gate, step_size, state_maps, decay_rate, skip_gain, norm_gain,
              queries, keys, values, source_len, *, dims):
    nx, ny, nz, T, em = dims
    nc = ny * nz
    vmem = pl.BlockSpec(memory_space=pltpu.VMEM)
    R = 2 * T
    DMA = pltpu.SemaphoreType.DMA
    out = jax.ShapeDtypeStruct((T, em), BF16)
    mo, ao = pl.pallas_call(
        functools.partial(section_kernel, dims),
        out_shape=(out, jax.ShapeDtypeStruct((T, ny * GROUP * D), BF16)),
        in_specs=[vmem] * 10 + [pl.BlockSpec(memory_space=pltpu.SMEM)],
        out_specs=(pl.BlockSpec(memory_space=pl.ANY), pl.BlockSpec(memory_space=pl.ANY)),
        scratch_shapes=[
            pltpu.VMEM((nz, 2, ny * T, D), BF16),
            pltpu.VMEM((ny, T, GROUP * D), BF16),
            pltpu.VMEM((nc, NST + 16, 128), BF16),
            pltpu.VMEM((nc, NST + 16, 128), BF16),
            pltpu.VMEM((nc, NST, 128), BF16),
            pltpu.VMEM((nc, NST, 128), BF16),
            pltpu.VMEM((T, em), F32),
            pltpu.VMEM((T, em), F32),
            pltpu.VMEM((T, em), F32),
            pltpu.VMEM((T, em), F32),
            pltpu.VMEM((em // HP, T), F32),
            pltpu.VMEM((em // HP, T), F32),
            pltpu.VMEM((T, T), F32),
            pltpu.VMEM((nz, R, ny * T), F32),
            pltpu.VMEM((R, T), jnp.int32),
            pltpu.VMEM((R, T), F32),
            pltpu.VMEM((R, T), F32),
            pltpu.VMEM((R, D), F32),
            pltpu.VMEM((ny, T, GROUP * D), BF16),
            pltpu.VMEM((T, em), BF16),
            pltpu.VMEM((T, 128), F32),
            pltpu.VMEM((T, 128), F32),
            DMA((ny, 2)), DMA((ny, 2)), DMA((ny,)), DMA((ny,)), DMA((3,)),
            DMA((2, nz, 2)), DMA((nz, 2)), DMA((nc,)), DMA((nc,)), DMA((nc,)), DMA((nc,)),
            DMA((ny,)), DMA((ny,)), DMA((max(1, em // 1024),)), DMA((max(1, em // 1024),)),
            DMA(()), DMA(()),
        ],
        compiler_params=pltpu.CompilerParams(
            collective_id=0, has_side_effects=True, vmem_limit_bytes=56 << 20
        ),
    )(
        mamba_input[0], mamba_gate[0], step_size[0], state_maps[0],
        decay_rate[None, :], jnp.repeat(skip_gain, HP)[None, :], norm_gain[None, :],
        queries[0], keys[0], values[0], source_len,
    )
    return mo[None], ao[None]


def solution(mesh):
    nx, nc = mesh.shape["segment"], mesh.shape["ctx"]
    nz = min(Z_RING, nc)
    placed = (
        P("segment", "ctx", "tp"), P("segment", "ctx", "tp"), P("segment", "ctx", "tp"),
        P("segment", "ctx", None), P("tp"), P("tp"), P("tp"),
        P("segment", "ctx", "tp"), P("segment", "ctx", "tp"), P("segment", "ctx", "tp"), P("segment"),
    )
    dims = (nx, nc // nz, nz, 128, 128 * nc)
    return jax.shard_map(
        functools.partial(on_device, dims=dims),
        mesh=mesh,
        in_specs=placed,
        out_specs=(P("segment", "ctx", "tp"), P("segment", "ctx", "tp")),
        check_vma=False,
    )
```

```python
import functools
import math

import jax
import jax.numpy as jnp
from jax import lax
from jax.experimental import pallas as pl
from jax.experimental.pallas import tpu as pltpu
from jax.sharding import PartitionSpec as P

QUERY_HEADS = 64
KEY_VALUE_HEADS = 8
GROUP = QUERY_HEADS // KEY_VALUE_HEADS
D = 128
NST = 128
HP = 64
Z_RING = 8
ORDER = (
    ("ring", 0), ("inner", 0, 1), ("ring", 1), ("inner", 1, 2), ("ring", 2), ("queries",), ("attend", 0),
    ("ring", 3), ("attend", 1), ("scan",), ("ring", 4), ("attend", 2), ("finish", 0, 1), ("attend", 3),
    ("finish", 1, 3), ("attend", 4), ("finish", 3, 4),
)
MESH = pl.DeviceIdType.MESH
NEG = -1e30
HIGH = lax.Precision.HIGHEST
F32 = jnp.float32
BF16 = jnp.bfloat16


def nt_dot(a, b):
    return lax.dot_general(a, b, (((1,), (1,)), ((), ())), preferred_element_type=F32)


def section_kernel(
    dims,
    x_hbm, gate_hbm, step_ref, maps_ref, rate_ref, skip_ref, q_hbm, k_hbm, v_hbm, src_ref,
    mo_ref, sq_ref, ao_ref,
    x_ref, gate_ref, srcs, srcb, kv, qb, sb, inbox, so, sin, yb, cum_e, ecum_e, tail_e, skip_e, cum_t, dt_t, gram,
    kt, mx, ls, acc, ob, gb, sqs,
    loc, src_send, src_recv, yk_send, yk_recv, q_send, q_recv, ring_send, ring_recv,
    s_send, s_recv, r_send, r_recv, ao_send, ao_recv, mo_send, mo_recv, sq_send, sq_recv,
):
    nx, ny, nz, T, em = dims
    nc = ny * nz
    seg = lax.axis_index("segment")
    me = lax.axis_index("ctx")
    tp = lax.axis_index("tp")
    y = me // nz
    z = lax.rem(me, nz)
    after = lax.rem(seg + 1, nx)
    before = lax.rem(seg + nx - 1, nx)
    half = nz // 2

    def remote(src, dst, ssem, rsem, dev):
        return pltpu.make_async_remote_copy(
            src_ref=src, dst_ref=dst, send_sem=ssem, recv_sem=rsem, device_id=dev, device_id_type=MESH
        )

    def at_ctx(c):
        return (seg, c, tp)

    load_x = pltpu.make_async_copy(x_hbm, x_ref, loc.at[0])
    load_gate = pltpu.make_async_copy(gate_hbm, gate_ref, loc.at[1])
    load_x.start()
    load_gate.start()

    barrier = pltpu.get_barrier_semaphore()
    for i in range(ny):
        pl.semaphore_signal(barrier, inc=1, device_id=(before, i * nz + z, tp), device_id_type=MESH)

    @pl.loop(1, nc)
    def _(i):
        pl.semaphore_signal(barrier, inc=1, device_id=at_ctx(lax.rem(me + i, nc)), device_id_type=MESH)

    pl.semaphore_signal(barrier, inc=1, device_id=(before, me, 1 - tp), device_id_type=MESH)

    def col(i, w):
        return pl.ds(pl.multiple_of(i * w, w), w)

    heads = em // HP
    row = lax.broadcasted_iota(jnp.int32, (T, T), 0)
    lane = lax.broadcasted_iota(jnp.int32, (T, T), 1)
    low = (row >= lane)
    dt = step_ref[...].astype(F32)
    logs = -rate_ref[...] * dt
    cum = jnp.dot(low.astype(F32), logs, precision=HIGH, preferred_element_type=F32)
    srcs[...] = jnp.full((8, 128), src_ref[0].astype(F32), F32)
    pl.semaphore_wait(barrier, nc - 1 + ny + 1)

    def src_copy():
        return remote(srcs, srcb, src_send, src_recv, (after, me, tp))

    def yk_copy(i, kvi, src):
        o = lax.rem(y + i, ny)
        return remote(
            src.at[:, col(o, D)], kv.at[z, kvi, pl.ds(pl.multiple_of(y * T, T), T)],
            yk_send.at[i, kvi], yk_recv.at[y, kvi], (after, o * nz + z, tp),
        )

    def q_copy(i):
        o = lax.rem(y + i, ny)
        return remote(
            q_hbm.at[:, col(o, GROUP * D)], qb.at[y], q_send.at[i], q_recv.at[y], (after, o * nz + z, tp)
        )

    for i in range(ny):
        yk_copy(i, 0, k_hbm).start()
        yk_copy(i, 1, v_hbm).start()
    src_copy().start()
    for i in range(ny):
        q_copy(i).start()

    def split3(a):
        hi = a.astype(BF16)
        rest = a - hi.astype(F32)
        mid = rest.astype(BF16)
        return [hi, mid, (rest - mid.astype(F32)).astype(BF16)]

    last = cum[T - 1:T, :]
    tail = jnp.exp(last - cum) * dt
    ecum = jnp.exp(cum)
    cum_t[...] = cum.T
    dt_t[...] = dt.T
    width = min(512, em)
    hrow = lax.broadcasted_iota(jnp.int32, (heads, width), 0) * HP
    hcol = lax.broadcasted_iota(jnp.int32, (heads, width), 1)

    def widen(values, put):
        stack = jnp.concatenate(split3(values), axis=1)
        for j in range(em // width):
            off = hcol + j * width - hrow
            pick = ((off >= 0) & (off < HP)).astype(F32).astype(BF16)
            wide = jnp.dot(stack, jnp.concatenate([pick] * 3, axis=0), preferred_element_type=F32)
            put(wide, slice(j * width, (j + 1) * width))

    def put_first(wide, sl):
        tail_e[:, sl] = wide[:T]
        ecum_e[:, sl] = wide[T:]

    def put_second(wide, sl):
        cum_e[:, sl] = wide[:T]
        skip_e[:, sl] = wide[T:T + 8]

    widen(jnp.concatenate([tail, ecum], axis=0), put_first)

    right = at_ctx(y * nz + lax.rem(z + 1, nz))
    left = at_ctx(y * nz + lax.rem(z + nz - 1, nz))

    def ring_copy(b, kvi, way):
        return remote(
            kv.at[b, kvi], kv.at[b, kvi], ring_send.at[way, b, kvi], ring_recv.at[b, kvi],
            right if way == 0 else left,
        )

    reach = [[half, half - 1], [half - 1, half]]

    def ring_step(s):
        for kvi in range(2):
            for way in range(2):
                b = lax.rem(z + nz - s, nz) if way == 0 else lax.rem(z + s, nz)
                if 0 < s <= reach[way][kvi]:
                    ring_copy(b, kvi, way).wait_recv()
                if s < reach[way][kvi]:
                    ring_copy(b, kvi, way).start()

    b_mat = maps_ref[:, :NST]
    c_mat = maps_ref[:, NST:]
    gram[...] = jnp.where(low, nt_dot(c_mat, b_mat), 0.0)
    b_t = b_mat.astype(F32).T.astype(BF16)
    sub16 = lax.broadcasted_iota(jnp.int32, (16, D), 0)

    def state_copy(i, p):
        return remote(sb.at[p], inbox.at[me], s_send.at[i], s_recv.at[me], at_ctx(p))

    def state_of(p):
        scaled = (x_ref[:, col(p, 128)].astype(F32) * tail_e[:, col(p, 128)]).astype(BF16)
        chunk = jnp.dot(b_t, scaled, preferred_element_type=F32)
        decay = ecum_e[T - 1:T, col(p, 128)]
        high = decay.astype(BF16).astype(F32)
        rest = jnp.where(sub16 < 8, high, decay - high)
        return chunk.astype(BF16), rest.astype(BF16)

    load_x.wait()

    @pl.loop(1, nc)
    def _(i):
        p = lax.rem(me + i, nc)
        chunk, rest = state_of(p)
        sb[p, 0:NST] = chunk
        sb[p, NST:NST + 16] = rest
        state_copy(i, p).start()

    chunk, rest = state_of(me)
    inbox[me, 0:NST] = chunk
    inbox[me, NST:NST + 16] = rest

    def wait_yk(c, kvi):
        remote(
            k_hbm.at[:, col(0, D)], kv.at[z, kvi, c * T:(c + 1) * T], yk_send.at[0, kvi], yk_recv.at[c, kvi],
            (after, me, tp),
        ).wait_recv()

    widen(jnp.concatenate([cum, jnp.broadcast_to(skip_ref[...], (16, heads))], axis=0), put_second)
    for c in range(ny):
        wait_yk(c, 0)
        wait_yk(c, 1)

    def inner(p):
        xt = x_ref[:, col(p, 128)]
        ce = cum_e[:, col(p, 128)]
        g = gram[...]
        outs = []
        for k in range(2):
            diff = ce[:, k * HP:k * HP + 1] - cum_t[pl.ds(2 * p + k, 1), :]
            w = g * jnp.exp(jnp.minimum(diff, 0.0)) * dt_t[pl.ds(2 * p + k, 1), :]
            outs.append(jnp.dot(w.astype(BF16), xt, preferred_element_type=F32))
        mixed = jnp.where(lane < HP, outs[0], outs[1])
        yb[:, col(p, 128)] = mixed + skip_e[0:1, col(p, 128)] * xt.astype(F32)

    def back_copy(c):
        return remote(so.at[c], sin.at[me], r_send.at[c], r_recv.at[me], at_ctx(c))

    def scan_step(c, carry):
        @pl.when(c != me)
        def _():
            remote(sb.at[0], inbox.at[c], s_send.at[0], s_recv.at[c], at_ctx(c)).wait_recv()
        so[c] = carry.astype(BF16)
        rest = inbox[c, NST:NST + 16].astype(F32)
        return carry * (rest[0:1] + rest[8:9]) + inbox[c, 0:NST].astype(F32)

    def scan():
        lax.fori_loop(0, nc, scan_step, jnp.zeros((NST, 128), F32))

        @pl.loop(1, nc)
        def _(i):
            back_copy(lax.rem(me + i, nc)).start()
        sin[me] = so[me]

    scale2 = 1.0 / math.sqrt(D) * math.log2(math.e)
    R = GROUP * T
    lane_t = lax.broadcasted_iota(jnp.int32, (1, T), 1)

    def attend_start():
        remote(srcs, srcb, src_send, src_recv, (after, me, tp)).wait_recv()
        for c in range(ny):
            remote(q_hbm.at[:, col(0, GROUP * D)], qb.at[c], q_send.at[0], q_recv.at[c], (after, me, tp)).wait_recv()
        mx[...] = jnp.full((ny, R, T), NEG, F32)
        ls[...] = jnp.zeros((ny, R, T), F32)
        acc[...] = jnp.zeros((ny, R, D), F32)

    def attend(blocks, final):
        n = len(blocks)
        keys = ny * T
        for i, b in enumerate(blocks):
            kt[:, i * keys:(i + 1) * keys] = kv[b, 0].T

        @pl.loop(0, ny)
        def _(c):
            pos = (row + (c * (nz * T) + z * T + 1)).astype(F32)
            lim = jnp.maximum(pos, srcb[0:1, :])
            lim = jnp.concatenate([lim] * GROUP, axis=0)
            q = jnp.concatenate([qb[c, :, g * D:(g + 1) * D] for g in range(GROUP)], axis=0)
            s = jnp.dot(q, kt[:, 0:n * keys], preferred_element_type=F32)
            parts = []
            top = None
            for i, b in enumerate(blocks):
                for j in range(ny):
                    part = s[:, i * keys + j * T:i * keys + (j + 1) * T]
                    if j > 0:
                        kpos = (lane_t + (j * (nz * T) + b * T)).astype(F32)
                        part = jnp.where(kpos < lim, part, NEG)
                    parts.append(part)
                    top = part if top is None else jnp.maximum(top, part)
            m_old = mx[c]
            m = jnp.maximum(m_old, jnp.max(top, axis=-1, keepdims=True))
            a = jnp.exp2((m_old - m) * scale2)
            mx[c] = m
            ws = [jnp.exp2((part - m) * scale2) for part in parts]
            total = ls[c] * a
            for w in ws:
                total = total + w
            w_all = jnp.concatenate([w.astype(BF16) for w in ws], axis=1)
            v_all = jnp.concatenate([kv[b, 1] for b in blocks], axis=0)
            o = acc[c] * a + jnp.dot(w_all, v_all, preferred_element_type=F32)
            if final:
                o = (o / jnp.sum(total, axis=-1, keepdims=True)).astype(BF16)
                for g in range(GROUP):
                    ob[c, :, g * D:(g + 1) * D] = o[g * T:(g + 1) * T]

                @pl.when(c != y)
                def _():
                    out_copy(c).start()

                @pl.when(c == y)
                def _():
                    own_out().start()
            else:
                ls[c] = total
                acc[c] = o

    def out_copy(c):
        return remote(ob.at[c], ao_ref.at[:, col(y, GROUP * D)], ao_send.at[c], ao_recv.at[y], at_ctx(c * nz + z))

    def own_out():
        return pltpu.make_async_copy(ob.at[y], ao_ref.at[:, col(y, GROUP * D)], loc.at[2])

    def sq_copy(other):
        return remote(
            sqs, sq_ref.at[tp], sq_send.at[other], sq_recv.at[tp], (after, me, lax.rem(tp + other, 2))
        )

    def gated_copy(p):
        return remote(
            gb.at[p], mo_ref.at[:, col(p, 128)], mo_send.at[p], mo_recv.at[p], (after, me, tp)
        )

    def finish_step(i):
        p = lax.rem(me + nc - i, nc)

        @pl.when(i > 0)
        def _():
            remote(so.at[0], sin.at[p], r_send.at[0], r_recv.at[p], at_ctx(p)).wait_recv()
        entered = jnp.dot(c_mat, sin[p], preferred_element_type=F32)
        raw = (yb[:, col(p, 128)] + ecum_e[:, col(p, 128)] * entered).astype(BF16).astype(F32)
        g = gate_ref[:, col(p, 128)].astype(F32)
        gated = raw * (g / (1.0 + jnp.exp(-g)))
        gb[p] = gated.astype(BF16)
        gated_copy(p).start()
        sqs[...] += gated * gated

    sqs[...] = jnp.zeros((T, 128), F32)
    load_gate.wait()

    def near(s):
        if s == 0 or s == half:
            return [lax.rem(z + s, nz)]
        return [lax.rem(z + nz - s, nz), lax.rem(z + s, nz)]

    quarter = nc // 4
    for item in ORDER:
        if item[0] == "ring":
            ring_step(item[1])
        elif item[0] == "inner":
            @pl.loop(item[1] * nc // 2, item[2] * nc // 2)
            def _(p):
                inner(p)
        elif item[0] == "queries":
            attend_start()
        elif item[0] == "attend":
            attend(near(item[1]), item[1] == half)
        elif item[0] == "scan":
            scan()
        else:
            @pl.loop(item[1] * quarter, item[2] * quarter)
            def _(i):
                finish_step(i)
            if item[2] == 4:
                for other in range(2):
                    sq_copy(other).start()

    for i in range(ny):
        yk_copy(i, 0, k_hbm).wait_send()
        yk_copy(i, 1, v_hbm).wait_send()
        q_copy(i).wait_send()
    src_copy().wait_send()
    for s in range(half):
        for kvi in range(2):
            for way in range(2):
                b = lax.rem(z + nz - s, nz) if way == 0 else lax.rem(z + s, nz)
                if s < reach[way][kvi]:
                    ring_copy(b, kvi, way).wait_send()

    @pl.loop(1, nc)
    def _(i):
        p = lax.rem(me + i, nc)
        state_copy(i, p).wait_send()
        back_copy(p).wait_send()

    own_out().wait()
    for i in range(1, ny):
        c = lax.rem(y + i, ny)
        out_copy(c).wait_send()
        remote(ob.at[0], ao_ref.at[:, col(c, GROUP * D)], ao_send.at[0], ao_recv.at[c], at_ctx(me)).wait_recv()

    @pl.loop(0, nc)
    def _(p):
        gated_copy(p).wait_send()
        gated_copy(p).wait_recv()
    for k in range(2):
        sq_copy(k).wait_send()
        remote(sqs, sq_ref.at[k], sq_send.at[k], sq_recv.at[k], (after, me, tp)).wait_recv()


def on_device(mamba_input, mamba_gate, step_size, state_maps, decay_rate, skip_gain, norm_gain,
              queries, keys, values, source_len, *, dims):
    nx, ny, nz, T, em = dims
    nc = ny * nz
    vmem = pl.BlockSpec(memory_space=pltpu.VMEM)
    hbm = pl.BlockSpec(memory_space=pl.ANY)
    R = GROUP * T
    DMA = pltpu.SemaphoreType.DMA
    out = jax.ShapeDtypeStruct((T, em), BF16)
    gated, squares, ao = pl.pallas_call(
        functools.partial(section_kernel, dims),
        out_shape=(
            out, jax.ShapeDtypeStruct((2, T, 128), F32), jax.ShapeDtypeStruct((T, ny * GROUP * D), BF16)
        ),
        in_specs=[hbm, hbm, vmem, vmem, vmem, vmem, hbm, hbm, hbm, pl.BlockSpec(memory_space=pltpu.SMEM)],
        out_specs=(hbm, hbm, hbm),
        scratch_shapes=[
            pltpu.VMEM((T, em), BF16),
            pltpu.VMEM((T, em), BF16),
            pltpu.VMEM((8, 128), F32),
            pltpu.VMEM((8, 128), F32),
            pltpu.VMEM((nz, 2, ny * T, D), BF16),
            pltpu.VMEM((ny, T, GROUP * D), BF16),
            pltpu.VMEM((nc, NST + 16, 128), BF16),
            pltpu.VMEM((nc, NST + 16, 128), BF16),
            pltpu.VMEM((nc, NST, 128), BF16),
            pltpu.VMEM((nc, NST, 128), BF16),
            pltpu.VMEM((T, em), F32),
            pltpu.VMEM((T, em), F32),
            pltpu.VMEM((T, em), F32),
            pltpu.VMEM((T, em), F32),
            pltpu.VMEM((8, em), F32),
            pltpu.VMEM((em // HP, T), F32),
            pltpu.VMEM((em // HP, T), F32),
            pltpu.VMEM((T, T), F32),
            pltpu.VMEM((D, 2 * ny * T), BF16),
            pltpu.VMEM((ny, R, T), F32),
            pltpu.VMEM((ny, R, T), F32),
            pltpu.VMEM((ny, R, D), F32),
            pltpu.VMEM((ny, T, GROUP * D), BF16),
            pltpu.VMEM((nc, T, 128), BF16),
            pltpu.VMEM((T, 128), F32),
            DMA((3,)), DMA(()), DMA(()),
            DMA((ny, 2)), DMA((ny, 2)), DMA((ny,)), DMA((ny,)),
            DMA((2, nz, 2)), DMA((nz, 2)), DMA((nc,)), DMA((nc,)), DMA((nc,)), DMA((nc,)),
            DMA((ny,)), DMA((ny,)), DMA((nc,)), DMA((nc,)), DMA((2,)), DMA((2,)),
        ],
        compiler_params=pltpu.CompilerParams(
            collective_id=0, has_side_effects=True, vmem_limit_bytes=56 << 20
        ),
    )(
        mamba_input[0], mamba_gate[0], step_size[0], state_maps[0],
        decay_rate[None, :], skip_gain[None, :],
        queries[0], keys[0], values[0], source_len,
    )
    total = jnp.sum(squares, axis=(0, 2))
    factor = lax.rsqrt(total / (2 * em) + 1e-5)[:, None]
    mo = (gated.astype(F32) * factor * norm_gain[None, :]).astype(BF16)
    return mo[None], ao[None]


def solution(mesh):
    nx, nc = mesh.shape["segment"], mesh.shape["ctx"]
    nz = min(Z_RING, nc)
    placed = (
        P("segment", "ctx", "tp"), P("segment", "ctx", "tp"), P("segment", "ctx", "tp"),
        P("segment", "ctx", None), P("tp"), P("tp"), P("tp"),
        P("segment", "ctx", "tp"), P("segment", "ctx", "tp"), P("segment", "ctx", "tp"), P("segment"),
    )
    dims = (nx, nc // nz, nz, 128, 128 * nc)
    return jax.shard_map(
        functools.partial(on_device, dims=dims),
        mesh=mesh,
        in_specs=placed,
        out_specs=(P("segment", "ctx", "tp"), P("segment", "ctx", "tp")),
        check_vma=False,
    )
```

```python
import functools
import math

import jax
import jax.numpy as jnp
from jax import lax
from jax.experimental import pallas as pl
from jax.experimental.pallas import tpu as pltpu
from jax.sharding import PartitionSpec as P

QUERY_HEADS = 64
KEY_VALUE_HEADS = 8
GROUP = QUERY_HEADS // KEY_VALUE_HEADS
D = 128
NST = 128
HP = 64
Z_RING = 8
STRIDE = 13
ORDER = (
    ("ring", 0), ("inner", 0, 1), ("ring", 1), ("inner", 1, 2), ("ring", 2), ("queries",),
    ("attend", 0), ("ring", 3), ("scan",), ("attend", 1), ("attend", 2), ("finish", 0, 1),
    ("attend", 3), ("finish", 1, 3), ("ring", 4), ("attend", 4), ("finish", 3, 4),
)
MESH = pl.DeviceIdType.MESH
NEG = -1e30
HIGH = lax.Precision.HIGHEST
F32 = jnp.float32
BF16 = jnp.bfloat16


def nt_dot(a, b):
    return lax.dot_general(a, b, (((1,), (1,)), ((), ())), preferred_element_type=F32)


def section_kernel(
    dims,
    x_hbm, gate_hbm, step_ref, maps_ref, rate_ref, skip_ref, q_hbm, k_hbm, v_hbm, src_ref,
    mo_ref, sq_ref, ao_ref,
    x_ref, gate_ref, srcs, srcb, kv, qb, sb, inbox, so, sin, yb, cum_e, ecum_e, tail_e, skip_e, cum_t, dt_t, gram,
    kt, mx, ls, acc, ob, gb, sqs,
    loc, src_send, src_recv, yk_send, yk_recv, q_send, q_recv, ring_send, ring_recv,
    s_send, s_recv, r_send, r_recv, ao_send, ao_recv, mo_send, mo_recv, sq_send, sq_recv,
):
    nx, ny, nz, T, em = dims
    nc = ny * nz
    seg = lax.axis_index("segment")
    me = lax.axis_index("ctx")
    tp = lax.axis_index("tp")
    y = me // nz
    z = lax.rem(me, nz)
    after = lax.rem(seg + 1, nx)
    before = lax.rem(seg + nx - 1, nx)
    half = nz // 2

    def remote(src, dst, ssem, rsem, dev):
        return pltpu.make_async_remote_copy(
            src_ref=src, dst_ref=dst, send_sem=ssem, recv_sem=rsem, device_id=dev, device_id_type=MESH
        )

    def at_ctx(c):
        return (seg, c, tp)

    load_x = pltpu.make_async_copy(x_hbm, x_ref, loc.at[0])
    load_gate = pltpu.make_async_copy(gate_hbm, gate_ref, loc.at[1])
    load_x.start()
    load_gate.start()

    barrier = pltpu.get_barrier_semaphore()
    for i in range(ny):
        pl.semaphore_signal(barrier, inc=1, device_id=(before, i * nz + z, tp), device_id_type=MESH)

    @pl.loop(1, nc)
    def _(i):
        pl.semaphore_signal(barrier, inc=1, device_id=at_ctx(lax.rem(me + i, nc)), device_id_type=MESH)

    pl.semaphore_signal(barrier, inc=1, device_id=(before, me, 1 - tp), device_id_type=MESH)

    def col(i, w):
        return pl.ds(pl.multiple_of(i * w, w), w)

    heads = em // HP
    row = lax.broadcasted_iota(jnp.int32, (T, T), 0)
    lane = lax.broadcasted_iota(jnp.int32, (T, T), 1)
    low = (row >= lane)
    dt = step_ref[...].astype(F32)
    logs = -rate_ref[...] * dt
    cum = jnp.dot(low.astype(F32), logs, precision=HIGH, preferred_element_type=F32)
    srcs[...] = jnp.full((8, 128), src_ref[0].astype(F32), F32)
    pl.semaphore_wait(barrier, nc - 1 + ny + 1)

    def src_copy():
        return remote(srcs, srcb, src_send, src_recv, (after, me, tp))

    def yk_copy(i, kvi, src):
        o = lax.rem(y + i, ny)
        return remote(
            src.at[:, col(o, D)], kv.at[z, kvi, pl.ds(pl.multiple_of(y * T, T), T)],
            yk_send.at[i, kvi], yk_recv.at[y, kvi], (after, o * nz + z, tp),
        )

    def q_copy(i):
        o = lax.rem(y + i, ny)
        return remote(
            q_hbm.at[:, col(o, GROUP * D)], qb.at[y], q_send.at[i], q_recv.at[y], (after, o * nz + z, tp)
        )

    for i in range(ny):
        yk_copy(i, 0, k_hbm).start()
        yk_copy(i, 1, v_hbm).start()
    src_copy().start()

    def split3(a):
        hi = a.astype(BF16)
        rest = a - hi.astype(F32)
        mid = rest.astype(BF16)
        return [hi, mid, (rest - mid.astype(F32)).astype(BF16)]

    last = cum[T - 1:T, :]
    tail = jnp.exp(last - cum) * dt
    ecum = jnp.exp(cum)
    cum_t[...] = cum.T
    dt_t[...] = dt.T
    width = min(512, em)
    hrow = lax.broadcasted_iota(jnp.int32, (heads, width), 0) * HP
    hcol = lax.broadcasted_iota(jnp.int32, (heads, width), 1)

    def widen(values, put):
        stack = jnp.concatenate(split3(values), axis=1)
        for j in range(em // width):
            off = hcol + j * width - hrow
            pick = ((off >= 0) & (off < HP)).astype(F32).astype(BF16)
            wide = jnp.dot(stack, jnp.concatenate([pick] * 3, axis=0), preferred_element_type=F32)
            put(wide, slice(j * width, (j + 1) * width))

    def put_first(wide, sl):
        tail_e[:, sl] = wide[:T]
        ecum_e[:, sl] = wide[T:]

    def put_second(wide, sl):
        cum_e[:, sl] = wide[:T]
        skip_e[:, sl] = wide[T:T + 8]

    widen(jnp.concatenate([tail, ecum], axis=0), put_first)

    right = at_ctx(y * nz + lax.rem(z + 1, nz))
    left = at_ctx(y * nz + lax.rem(z + nz - 1, nz))

    def ring_copy(b, kvi, way):
        return remote(
            kv.at[b, kvi], kv.at[b, kvi], ring_send.at[way, b, kvi], ring_recv.at[b, kvi],
            right if way == 0 else left,
        )

    reach = [[half, half - 1], [half - 1, half]]

    def ring_step(s):
        for kvi in range(2):
            for way in range(2):
                b = lax.rem(z + nz - s, nz) if way == 0 else lax.rem(z + s, nz)
                if 0 < s <= reach[way][kvi]:
                    ring_copy(b, kvi, way).wait_recv()
                if s < reach[way][kvi]:
                    ring_copy(b, kvi, way).start()

    b_mat = maps_ref[:, :NST]
    c_mat = maps_ref[:, NST:]
    gram[...] = jnp.where(low, nt_dot(c_mat, b_mat), 0.0)
    b_t = b_mat.astype(F32).T.astype(BF16)
    sub16 = lax.broadcasted_iota(jnp.int32, (16, D), 0)

    def state_copy(i, p):
        return remote(sb.at[p], inbox.at[me], s_send.at[i], s_recv.at[me], at_ctx(p))

    def state_of(p):
        scaled = (x_ref[:, col(p, 128)].astype(F32) * tail_e[:, col(p, 128)]).astype(BF16)
        chunk = jnp.dot(b_t, scaled, preferred_element_type=F32)
        decay = ecum_e[T - 1:T, col(p, 128)]
        high = decay.astype(BF16).astype(F32)
        rest = jnp.where(sub16 < 8, high, decay - high)
        return chunk.astype(BF16), rest.astype(BF16)

    load_x.wait()

    @pl.loop(1, nc)
    def _(i):
        p = lax.rem(me + i * STRIDE, nc)
        chunk, rest = state_of(p)
        sb[p, 0:NST] = chunk
        sb[p, NST:NST + 16] = rest
        state_copy(i, p).start()

        @pl.when(lax.rem(i, nc // ny) == 0)
        def _():
            q_copy(i // (nc // ny) - 1).start()

    q_copy(ny - 1).start()

    chunk, rest = state_of(me)
    inbox[me, 0:NST] = chunk
    inbox[me, NST:NST + 16] = rest

    def wait_yk(c, kvi):
        remote(
            k_hbm.at[:, col(0, D)], kv.at[z, kvi, c * T:(c + 1) * T], yk_send.at[0, kvi], yk_recv.at[c, kvi],
            (after, me, tp),
        ).wait_recv()

    widen(jnp.concatenate([cum, jnp.broadcast_to(skip_ref[...], (16, heads))], axis=0), put_second)
    for c in range(ny):
        wait_yk(c, 0)
        wait_yk(c, 1)

    def inner(p):
        xt = x_ref[:, col(p, 128)]
        ce = cum_e[:, col(p, 128)]
        g = gram[...]
        outs = []
        for k in range(2):
            diff = ce[:, k * HP:k * HP + 1] - cum_t[pl.ds(2 * p + k, 1), :]
            w = g * jnp.exp(jnp.minimum(diff, 0.0)) * dt_t[pl.ds(2 * p + k, 1), :]
            outs.append(jnp.dot(w.astype(BF16), xt, preferred_element_type=F32))
        mixed = jnp.where(lane < HP, outs[0], outs[1])
        yb[:, col(p, 128)] = mixed + skip_e[0:1, col(p, 128)] * xt.astype(F32)

    def back_copy(c):
        return remote(so.at[c], sin.at[me], r_send.at[c], r_recv.at[me], at_ctx(c))

    def scan_step(c, carry):
        @pl.when(c != me)
        def _():
            remote(sb.at[0], inbox.at[c], s_send.at[0], s_recv.at[c], at_ctx(c)).wait_recv()
        so[c] = carry.astype(BF16)
        rest = inbox[c, NST:NST + 16].astype(F32)
        return carry * (rest[0:1] + rest[8:9]) + inbox[c, 0:NST].astype(F32)

    def scan():
        lax.fori_loop(0, nc, scan_step, jnp.zeros((NST, 128), F32))

        @pl.loop(1, nc)
        def _(i):
            back_copy(lax.rem(me + i * STRIDE, nc)).start()
        sin[me] = so[me]

    scale2 = 1.0 / math.sqrt(D) * math.log2(math.e)
    R = GROUP * T
    lane_t = lax.broadcasted_iota(jnp.int32, (1, T), 1)

    def attend_start():
        remote(srcs, srcb, src_send, src_recv, (after, me, tp)).wait_recv()
        for c in range(ny):
            remote(q_hbm.at[:, col(0, GROUP * D)], qb.at[c], q_send.at[0], q_recv.at[c], (after, me, tp)).wait_recv()
        mx[...] = jnp.full((ny, R, T), NEG, F32)
        ls[...] = jnp.zeros((ny, R, T), F32)
        acc[...] = jnp.zeros((ny, R, D), F32)

    def attend(blocks, final):
        n = len(blocks)
        keys = ny * T
        for i, b in enumerate(blocks):
            kt[:, i * keys:(i + 1) * keys] = kv[b, 0].T

        @pl.loop(0, ny)
        def _(c):
            pos = (row + (c * (nz * T) + z * T + 1)).astype(F32)
            lim = jnp.maximum(pos, srcb[0:1, :])
            lim = jnp.concatenate([lim] * GROUP, axis=0)
            q = jnp.concatenate([qb[c, :, g * D:(g + 1) * D] for g in range(GROUP)], axis=0)
            s = jnp.dot(q, kt[:, 0:n * keys], preferred_element_type=F32)
            parts = []
            top = None
            for i, b in enumerate(blocks):
                for j in range(ny):
                    part = s[:, i * keys + j * T:i * keys + (j + 1) * T]
                    if j > 0:
                        kpos = (lane_t + (j * (nz * T) + b * T)).astype(F32)
                        part = jnp.where(kpos < lim, part, NEG)
                    parts.append(part)
                    top = part if top is None else jnp.maximum(top, part)
            m_old = mx[c]
            m = jnp.maximum(m_old, jnp.max(top, axis=-1, keepdims=True))
            a = jnp.exp2((m_old - m) * scale2)
            mx[c] = m
            ws = [jnp.exp2((part - m) * scale2) for part in parts]
            total = ls[c] * a
            for w in ws:
                total = total + w
            w_all = jnp.concatenate([w.astype(BF16) for w in ws], axis=1)
            v_all = jnp.concatenate([kv[b, 1] for b in blocks], axis=0)
            o = acc[c] * a + jnp.dot(w_all, v_all, preferred_element_type=F32)
            if final:
                o = (o / jnp.sum(total, axis=-1, keepdims=True)).astype(BF16)
                for g in range(GROUP):
                    ob[c, :, g * D:(g + 1) * D] = o[g * T:(g + 1) * T]

                @pl.when(c != y)
                def _():
                    out_copy(c).start()

                @pl.when(c == y)
                def _():
                    own_out().start()
            else:
                ls[c] = total
                acc[c] = o

    def out_copy(c):
        return remote(ob.at[c], ao_ref.at[:, col(y, GROUP * D)], ao_send.at[c], ao_recv.at[y], at_ctx(c * nz + z))

    def own_out():
        return pltpu.make_async_copy(ob.at[y], ao_ref.at[:, col(y, GROUP * D)], loc.at[2])

    def sq_copy(other):
        return remote(
            sqs, sq_ref.at[tp], sq_send.at[other], sq_recv.at[tp], (after, me, lax.rem(tp + other, 2))
        )

    def gated_copy(p):
        return remote(
            gb.at[p], mo_ref.at[:, col(p, 128)], mo_send.at[p], mo_recv.at[p], (after, me, tp)
        )

    def finish_step(i):
        p = lax.rem(me + (nc - i) * STRIDE, nc)

        @pl.when(i > 0)
        def _():
            remote(so.at[0], sin.at[p], r_send.at[0], r_recv.at[p], at_ctx(p)).wait_recv()
        entered = jnp.dot(c_mat, sin[p], preferred_element_type=F32)
        raw = (yb[:, col(p, 128)] + ecum_e[:, col(p, 128)] * entered).astype(BF16).astype(F32)
        g = gate_ref[:, col(p, 128)].astype(F32)
        gated = raw * (g / (1.0 + jnp.exp(-g)))
        gb[p] = gated.astype(BF16)
        gated_copy(p).start()
        sqs[...] += gated * gated

    sqs[...] = jnp.zeros((T, 128), F32)
    load_gate.wait()

    def near(s):
        if s == 0 or s == half:
            return [lax.rem(z + s, nz)]
        return [lax.rem(z + nz - s, nz), lax.rem(z + s, nz)]

    quarter = nc // 4
    for item in ORDER:
        if item[0] == "ring":
            ring_step(item[1])
        elif item[0] == "inner":
            @pl.loop(item[1] * nc // 2, item[2] * nc // 2)
            def _(p):
                inner(p)
        elif item[0] == "queries":
            attend_start()
        elif item[0] == "attend":
            attend(near(item[1]), item[1] == half)
        elif item[0] == "scan":
            scan()
        else:
            @pl.loop(item[1] * quarter, item[2] * quarter)
            def _(i):
                finish_step(i)
            if item[2] == 4:
                sqs[...] = jnp.broadcast_to(jnp.sum(sqs[...], axis=-1, keepdims=True), (T, 128))
                for other in range(2):
                    sq_copy(other).start()

    for i in range(ny):
        yk_copy(i, 0, k_hbm).wait_send()
        yk_copy(i, 1, v_hbm).wait_send()
        q_copy(i).wait_send()
    src_copy().wait_send()
    for s in range(half):
        for kvi in range(2):
            for way in range(2):
                b = lax.rem(z + nz - s, nz) if way == 0 else lax.rem(z + s, nz)
                if s < reach[way][kvi]:
                    ring_copy(b, kvi, way).wait_send()

    @pl.loop(1, nc)
    def _(i):
        p = lax.rem(me + i, nc)
        state_copy(i, p).wait_send()
        back_copy(p).wait_send()

    own_out().wait()
    for i in range(1, ny):
        c = lax.rem(y + i, ny)
        out_copy(c).wait_send()
        remote(ob.at[0], ao_ref.at[:, col(c, GROUP * D)], ao_send.at[0], ao_recv.at[c], at_ctx(me)).wait_recv()

    @pl.loop(0, nc)
    def _(p):
        gated_copy(p).wait_send()
        gated_copy(p).wait_recv()
    for k in range(2):
        sq_copy(k).wait_send()
        remote(sqs, sq_ref.at[k], sq_send.at[k], sq_recv.at[k], (after, me, tp)).wait_recv()


def on_device(mamba_input, mamba_gate, step_size, state_maps, decay_rate, skip_gain, norm_gain,
              queries, keys, values, source_len, *, dims):
    nx, ny, nz, T, em = dims
    nc = ny * nz
    vmem = pl.BlockSpec(memory_space=pltpu.VMEM)
    hbm = pl.BlockSpec(memory_space=pl.ANY)
    R = GROUP * T
    DMA = pltpu.SemaphoreType.DMA
    out = jax.ShapeDtypeStruct((T, em), BF16)
    gated, squares, ao = pl.pallas_call(
        functools.partial(section_kernel, dims),
        out_shape=(
            out, jax.ShapeDtypeStruct((2, T, 128), F32), jax.ShapeDtypeStruct((T, ny * GROUP * D), BF16)
        ),
        in_specs=[hbm, hbm, vmem, vmem, vmem, vmem, hbm, hbm, hbm, pl.BlockSpec(memory_space=pltpu.SMEM)],
        out_specs=(hbm, hbm, hbm),
        scratch_shapes=[
            pltpu.VMEM((T, em), BF16),
            pltpu.VMEM((T, em), BF16),
            pltpu.VMEM((8, 128), F32),
            pltpu.VMEM((8, 128), F32),
            pltpu.VMEM((nz, 2, ny * T, D), BF16),
            pltpu.VMEM((ny, T, GROUP * D), BF16),
            pltpu.VMEM((nc, NST + 16, 128), BF16),
            pltpu.VMEM((nc, NST + 16, 128), BF16),
            pltpu.VMEM((nc, NST, 128), BF16),
            pltpu.VMEM((nc, NST, 128), BF16),
            pltpu.VMEM((T, em), F32),
            pltpu.VMEM((T, em), F32),
            pltpu.VMEM((T, em), F32),
            pltpu.VMEM((T, em), F32),
            pltpu.VMEM((8, em), F32),
            pltpu.VMEM((em // HP, T), F32),
            pltpu.VMEM((em // HP, T), F32),
            pltpu.VMEM((T, T), F32),
            pltpu.VMEM((D, 2 * ny * T), BF16),
            pltpu.VMEM((ny, R, T), F32),
            pltpu.VMEM((ny, R, T), F32),
            pltpu.VMEM((ny, R, D), F32),
            pltpu.VMEM((ny, T, GROUP * D), BF16),
            pltpu.VMEM((nc, T, 128), BF16),
            pltpu.VMEM((T, 128), F32),
            DMA((3,)), DMA(()), DMA(()),
            DMA((ny, 2)), DMA((ny, 2)), DMA((ny,)), DMA((ny,)),
            DMA((2, nz, 2)), DMA((nz, 2)), DMA((nc,)), DMA((nc,)), DMA((nc,)), DMA((nc,)),
            DMA((ny,)), DMA((ny,)), DMA((nc,)), DMA((nc,)), DMA((2,)), DMA((2,)),
        ],
        compiler_params=pltpu.CompilerParams(
            collective_id=0, has_side_effects=True, vmem_limit_bytes=56 << 20
        ),
    )(
        mamba_input[0], mamba_gate[0], step_size[0], state_maps[0],
        decay_rate[None, :], skip_gain[None, :],
        queries[0], keys[0], values[0], source_len,
    )
    factor = lax.rsqrt((squares[0, :, :1] + squares[1, :, :1]) / (2 * em) + 1e-5)
    mo = (gated.astype(F32) * factor * norm_gain[None, :]).astype(BF16)
    return mo[None], ao[None]


def solution(mesh):
    nx, nc = mesh.shape["segment"], mesh.shape["ctx"]
    nz = min(Z_RING, nc)
    placed = (
        P("segment", "ctx", "tp"), P("segment", "ctx", "tp"), P("segment", "ctx", "tp"),
        P("segment", "ctx", None), P("tp"), P("tp"), P("tp"),
        P("segment", "ctx", "tp"), P("segment", "ctx", "tp"), P("segment", "ctx", "tp"), P("segment"),
    )
    dims = (nx, nc // nz, nz, 128, 128 * nc)
    return jax.shard_map(
        functools.partial(on_device, dims=dims),
        mesh=mesh,
        in_specs=placed,
        out_specs=(P("segment", "ctx", "tp"), P("segment", "ctx", "tp")),
        check_vma=False,
    )
```
